256 devices in a mesh: rep: 16 (over z, y_hi), exp: 16 (over y_lo, x, core).
Axes of the slice: x: 4, y: 4 (y_hi: 2, y_lo: 2; y = y_hi * 2 + y_lo), z: 8, core: 2. Of those that a mesh axis runs over, the one named last changes fastest.
Arguments:
- tokens: bfloat16 [8192, 2048], P(('rep', 'exp')), may hold values from -6 to 6
- attend_weight: bfloat16 [2048, 16, 256], P(None, 'exp'), may hold values from -0.125 to 0.125
- value_weight: bfloat16 [2048, 32, 256], P(None, 'exp'), may hold values from -0.125 to 0.125
- rate_weight: bfloat16 [2048, 32, 2], P(None, 'exp'), may hold values from -0.125 to 0.125
- decay_rate: float32 [32], P('exp'), may hold values from 0.002 to 0.2
- output_weight: bfloat16 [32, 128, 2048], P('exp'), may hold values from -0.09375 to 0.09375
- state_cache: float32 [128, 32, 128, 128], P('rep', 'exp'), may hold values from -2.4 to 2.4
- resume_from: int32 [128], replicated, may hold values from 0 to 127, as said below
- expert_index: int32 [8192, 10], P(('rep', 'exp')), may hold values from 0 to 15, all different within a row; in each aligned block of 32 rows (0 to 31, 32 to 63, ...) at most 32 rows name the same one
- route_weight: float32 [8192, 10], P(('rep', 'exp')), may hold values from 0.02 to 0.3
- expert_inner: bfloat16 [16, 2048, 1024], P('exp'), may hold values from -0.125 to 0.125
- expert_outer: bfloat16 [16, 512, 2048], P('exp'), may hold values from -0.25 to 0.25
Outputs:
- layer_output: bfloat16 [8192, 2048], P(('rep', 'exp'))
- final_state: float32 [128, 32, 128, 128], P('rep', 'exp')
The draws below stay inside these ranges and needn't reach their ends.
Inputs may be any that keep to these rules, and one draw needn't show every extreme that they name: `resume_from`: entry r * 8 + b is the cache row of trajectory b of group r; cache row c belongs to group c // 8. The 8 trajectories of one group take their rows from 8 different groups; a row may serve several groups. `expert_index`: each row names 10 different experts.
All inputs are finite; a program needn't handle non-finite values.
Results may differ from the reference program's by a relative error of at most 0.013.
Values may be sent and summed in bfloat16 or wider, within the bound.
No kernel may reach another device: no remote copies, remote signals or barrier semaphores. Data moves between devices by JAX's collectives and lax.ppermute only.
A program may use at most 128 MiB of HBM per device.

```python
import math
import jax
import jax.numpy as jnp
import numpy as np
from jax import lax

D = 2048
KHEADS = 16
VHEADS = 32
DK = 128
DV = 128
MI = 512
TRAJ = 8
LEN = 64
EXPERTS = 16
TOP = 10
ROWS = 32
TOKENS = 8192
N_REP = 16


def draw_resume_from(key, part):
    favoured = (jax.random.randint(jax.random.fold_in(key, 7), (N_REP,), 0, 4) == 0).astype(jnp.int32)

    def one_group(number):
        group_key = jax.random.fold_in(jax.random.fold_in(key, 11), number)
        key_order, key_place, key_slot = jax.random.split(group_key, 3)
        scores = jax.random.randint(key_order, (N_REP,), 0, 1000) - 700 * favoured
        ranking = jnp.argsort(scores * N_REP + jnp.arange(N_REP, dtype=jnp.int32))
        sources = ranking[:TRAJ].astype(jnp.int32)
        sources = sources[jax.random.permutation(key_place, TRAJ)]
        slot_rows = jax.random.randint(key_slot, (TRAJ,), 0, TRAJ)
        return (sources * TRAJ + slot_rows).astype(jnp.int32)
    return jax.vmap(one_group)(jnp.arange(N_REP, dtype=jnp.int32)).reshape(-1)


def shard_levels(stream_key, extent, cuts, low, largest):
    factor_of, own = 1.0, jax.random.fold_in(stream_key, 6)
    for axis_at, parts in cuts:
        heights = jnp.exp(jax.random.uniform(jax.random.fold_in(own, axis_at), (parts,), jnp.float32, low / len(cuts), largest / len(cuts)))
        factor_of = factor_of * jnp.repeat(heights, extent[axis_at] // parts).reshape([-1 if axis == axis_at else 1 for axis in range(len(extent))])
    return factor_of


def routed_block(own_key, own, number, rows, count, top, reach, lean):
    order = jax.random.permutation(own_key, count)
    heavy_load, usual = load_shares(count, rows * top, reach, lean, True), load_shares(count, rows * top, reach, lean, False)
    places = jnp.arange(count)

    def named(sizes, turn):
        used = int((sizes > 0).sum())
        fixed = max(1, used // 4)
        passed = fixed + (places - fixed + turn * (used - fixed)) % max(1, count - fixed)
        return jnp.zeros((count,), jnp.int32).at[order[jnp.where(places < fixed, places, passed)]].set(jnp.asarray(sizes, jnp.int32))

    sizes = jnp.where(number % 4 == 0, named(heavy_load, number // 4), named(usual, number - number // 4 - 1))
    mixed = jax.random.permutation(jax.random.fold_in(own, 3), count)
    source_of, receiver = mixed[0:count // 2 * 2:2], mixed[1:count // 2 * 2:2]
    room = jnp.minimum(sizes[source_of] - 1, reach - sizes[receiver]) // 2
    room = jnp.where((source_of == order[0]) | (receiver == order[0]) | (sizes[receiver] == 0), 0, jnp.maximum(room, 0))
    passed = jax.random.randint(jax.random.fold_in(own, 4), (count // 2,), 0, 1 << 20) % (room + 1)
    sizes = sizes.at[source_of].add(-passed).at[receiver].add(passed)
    labels = jnp.searchsorted(jnp.cumsum(sizes), jnp.arange(rows * top), side="right").astype(jnp.int32)
    table = labels.reshape(top, rows).T
    table = table[jax.random.permutation(jax.random.fold_in(own, 1), rows)]
    turn = jax.random.randint(jax.random.fold_in(own, 2), (rows, 1), 0, top)
    return jnp.take_along_axis(table, (jnp.arange(top)[None, :] + turn) % top, axis=1)


def load_shares(count, total, bound, slope, full):
    loads = [(1 << 20) // math.isqrt(rank ** slope) + 1 for rank in range(1, count + 1)]
    largest = bound if full else min(bound, max(-(-total // count), total * loads[0] // sum(loads)))
    least = 1 if total - largest >= count - 1 else 0
    given, rest = [largest] + [least] * (count - 1), total - largest - least * (count - 1)
    while rest > 0:
        candidates = [i for i in range(1, count) if given[i] < largest] or [i for i in range(1, count) if given[i] < bound]
        pool, budget = sum([loads[i] for i in candidates]), rest
        for i in candidates:
            extra = min(bound - given[i], max(1, budget * loads[i] // pool), rest)
            given[i] = given[i] + extra
            rest = rest - extra
    return np.array(given)


def gaussian(own_key, shape, spread, reach, cuts=(), kind=jnp.bfloat16):
    array = jax.random.normal(own_key, shape, jnp.float32) * spread
    if len(cuts) > 0:
        array = shard_levels(own_key, shape, cuts, -0.22, 0.18) * array
    return jnp.clip(array, min=-reach, max=reach).astype(kind)


def setup_inputs(seed: int = 0) -> dict:
    splits = jax.random.split(jax.random.key(seed), 13)
    tokens = gaussian(splits[0], (TOKENS, D), 1.0, 6.0, ((0, 256),))
    attend_weight = gaussian(splits[1], (D, KHEADS, 2 * DK), D ** -0.5, 0.125, ((1, 16),))
    value_weight = gaussian(splits[2], (D, VHEADS, 2 * DV), D ** -0.5, 0.125, ((1, 16),))
    rate_weight = gaussian(splits[3], (D, VHEADS, 2), D ** -0.5, 0.125, ((1, 16),))
    decay_rate = jnp.clip(jnp.exp(math.log(0.2) - 4.6051702 * jax.random.uniform(splits[4], (VHEADS,), jnp.float32) ** shard_levels(splits[4], (VHEADS,), ((0, 16),), -0.2, 0.2)), 0.002, 0.2)
    output_weight = gaussian(splits[5], (VHEADS, DV, D), (VHEADS * DV) ** -0.5, 0.09375, ((0, 16),))
    state_cache = gaussian(splits[6], (N_REP * TRAJ, VHEADS, DV, DK), 0.3, 2.4, ((0, 16), (1, 16)), jnp.float32)
    resume_from = draw_resume_from(jax.random.fold_in(splits[12], 71), 0)
    expert_index_keys = jax.random.split(jax.random.fold_in(splits[8], 1), TOKENS // ROWS)
    expert_index_turns = jax.random.permutation(jax.random.fold_in(splits[8], 3), TOKENS // ROWS)
    expert_index = jax.vmap(lambda own, number: routed_block(jax.random.fold_in(splits[8], 2), own, number, ROWS, EXPERTS, TOP, ROWS, 2))(expert_index_keys, expert_index_turns).reshape((TOKENS, TOP))
    route_weight = jnp.clip(jnp.exp(math.log(0.3) - 2.7080503 * jax.random.uniform(splits[9], (TOKENS, TOP), jnp.float32) ** shard_levels(splits[9], (TOKENS, TOP), ((0, 256),), -0.2, 0.2)), 0.02, 0.3)
    expert_inner = gaussian(splits[10], (EXPERTS, D, 2 * MI), D ** -0.5, 0.125, ((0, 16),))
    expert_outer = gaussian(splits[11], (EXPERTS, MI, D), MI ** -0.5, 0.25, ((0, 16),))
    return dict(tokens=tokens, attend_weight=attend_weight, value_weight=value_weight, rate_weight=rate_weight, decay_rate=decay_rate, output_weight=output_weight, state_cache=state_cache, resume_from=resume_from, expert_index=expert_index, route_weight=route_weight, expert_inner=expert_inner, expert_outer=expert_outer)


EPSILON = 1e-06
HIGHEST = lax.Precision.HIGHEST

def rms_scale(values):
    return values * lax.rsqrt(lax.optimization_barrier(jnp.mean(values * values, axis=-1, keepdims=True)) + EPSILON)

def unit_length(values):
    return values * lax.rsqrt(lax.optimization_barrier(jnp.sum(values * values, axis=-1, keepdims=True)) + EPSILON)

def head_inputs(attend_part, value_part, rate_part, key_heads, value_heads, decay_rate):
    count = attend_part.shape[0]
    key_size = attend_part.shape[1] // (2 * key_heads)
    value_size = value_part.shape[1] // (2 * value_heads)
    paired = attend_part.reshape(count, key_heads, 2, key_size)
    repeat = value_heads // key_heads
    query = jnp.repeat(unit_length(paired[:, :, 0]), repeat, axis=1) * key_size ** (-0.5)
    key_rows = jnp.repeat(unit_length(paired[:, :, 1]), repeat, axis=1)
    value_pair = value_part.reshape(count, value_heads, 2, value_size)
    rate_pair = rate_part.reshape(count, value_heads, 2)
    beta_rows = jax.nn.sigmoid(rate_pair[:, :, 1])
    log_decay = -decay_rate[None, :] * jax.nn.softplus(rate_pair[:, :, 0])
    return (query, key_rows, value_pair[:, :, 0], value_pair[:, :, 1], beta_rows, log_decay)

def reference(tokens, attend_weight, value_weight, rate_weight, decay_rate, output_weight, state_cache, resume_from, expert_index, route_weight, expert_inner, expert_outer):
    model = tokens.shape[1]
    key_heads = attend_weight.shape[1]
    value_heads = value_weight.shape[1]
    residual = tokens.astype(jnp.float32)
    normed = rms_scale(residual).astype(jnp.bfloat16)
    attend_part = jnp.dot(normed, attend_weight.reshape(model, -1), preferred_element_type=jnp.float32)
    value_part = jnp.dot(normed, value_weight.reshape(model, -1), preferred_element_type=jnp.float32)
    rate_part = jnp.dot(normed, rate_weight.reshape(model, -1), preferred_element_type=jnp.float32)
    query, key_rows, value_rows, gate_rows, beta_rows, log_decay = head_inputs(attend_part, value_part, rate_part, key_heads, value_heads, decay_rate)
    trajectories = N_REP * TRAJ

    def regroup(values):
        return values.reshape((trajectories, LEN) + values.shape[1:])
    start = jnp.take(state_cache, resume_from, axis=0)

    def one_trajectory(packed):
        query_t, key_t, value_t, beta_t, decay_t, state = packed

        def advance(carry, item):
            query_s, key_s, value_s, beta_s, decay_s = item
            carry = jnp.exp(decay_s)[:, None, None] * carry
            predicted = jnp.einsum('hvk,hk->hv', carry, key_s, precision=HIGHEST)
            carry = carry + (beta_s[:, None] * (value_s - predicted))[:, :, None] * key_s[:, None, :]
            return (carry, jnp.einsum('hvk,hk->hv', carry, query_s, precision=HIGHEST))
        return lax.scan(advance, state, (query_t, key_t, value_t, beta_t, decay_t))
    final_state, readout = lax.map(one_trajectory, (regroup(query), regroup(key_rows), regroup(value_rows), regroup(beta_rows), regroup(log_decay), start))
    readout = readout.reshape(value_rows.shape)
    gated = (rms_scale(readout) * jax.nn.silu(gate_rows)).astype(jnp.bfloat16).reshape(readout.shape[0], -1)
    attended = jnp.dot(gated, output_weight.reshape(-1, model), preferred_element_type=jnp.float32)
    hidden = residual + attended
    hidden_normed = rms_scale(hidden).astype(jnp.bfloat16)
    inner = expert_outer.shape[1]

    def add_expert(total, packed):
        inner_matrix, outer_matrix, number = packed
        share = lax.optimization_barrier(jnp.sum(jnp.where(expert_index == number, route_weight, jnp.zeros_like(route_weight)), axis=1))
        both_parts = jnp.dot(hidden_normed, inner_matrix, preferred_element_type=jnp.float32)
        activated = (jax.nn.silu(both_parts[:, :inner]) * both_parts[:, inner:]).astype(jnp.bfloat16)
        produced = jnp.dot(activated, outer_matrix, preferred_element_type=jnp.float32).astype(jnp.bfloat16)
        return (total + share[:, None] * produced.astype(jnp.float32), None)
    numbers = jnp.arange(expert_inner.shape[0], dtype=jnp.int32)
    expert_sum, unused = lax.scan(add_expert, jnp.zeros(hidden.shape, jnp.float32), (expert_inner, expert_outer, numbers))
    layer_output = (hidden + expert_sum).astype(jnp.bfloat16)
    return (layer_output, final_state)
```

```python
import jax
import jax.numpy as jnp
from jax import lax
from jax.experimental import pallas as pl
from jax.experimental.pallas import tpu as pltpu
from jax.sharding import PartitionSpec as P


EPSILON = 1e-06
HIGHEST = lax.Precision.HIGHEST
F32 = jnp.float32
BF16 = jnp.bfloat16

NY, NX, NC = 2, 4, 2


def place(y, x, c):
    return (y * NX + x) * NC + c


SWAP = [(i, i ^ 1) for i in range(NY * NX * NC)]


def spread(dx):
    return [
        (place(y, x, c), place(y ^ c, (x + dx) % NX, y))
        for y in range(NY)
        for x in range(NX)
        for c in range(NC)
    ]


def collect(dx):
    return [(b, a) for a, b in spread(dx)]


def rms_scale(values):
    return values * lax.rsqrt(jnp.mean(values * values, axis=-1, keepdims=True) + EPSILON)


def halves(values):
    high = values.astype(BF16)
    return high, (values - high.astype(F32)).astype(BF16)


def left(values):
    high, low = halves(values)
    return jnp.concatenate([high, low, high], axis=1)


def right(values, axis=0):
    high, low = halves(values)
    return jnp.concatenate([high, high, low], axis=axis)


def dot(a, b, dims=((1,), (0,))):
    return lax.dot_general(a, b, (dims, ((), ())), preferred_element_type=F32)


def send_kernel(resume_ref, me_ref, cache_ref, out_ref):
    trajs = cache_ref.shape[0]
    for slot in range(out_ref.shape[0]):
        row = jnp.int32(0)
        for place_of in range(trajs):
            value = resume_ref[slot * trajs + place_of]
            row = jnp.where(value // trajs == me_ref[0], value % trajs, row)
        out_ref[slot] = cache_ref[row].astype(BF16)


def chunk_kernel(
    decay_own_ref, decay_other_ref, seen_ref, attend_own_ref, value_own_ref, rate_own_ref,
    attend_other_ref, value_other_ref, rate_other_ref,
    mix_ref, base_ref, key_ref, close_ref, gate_ref, proj_ref, rate_ref,
):
    width = 64
    row = lax.broadcasted_iota(jnp.int32, (width, width), 0)
    col = lax.broadcasted_iota(jnp.int32, (width, width), 1)
    row3 = lax.broadcasted_iota(jnp.int32, (width, 3 * width), 0)
    col3 = lax.broadcasted_iota(jnp.int32, (width, 3 * width), 1) % width
    lower3 = (col3 <= row3).astype(F32).astype(BF16)
    eye = (col == row).astype(F32)
    lane = lax.broadcasted_iota(jnp.int32, (1, 128), 1)
    decays = [
        jnp.where(lane == 0, ref[0], jnp.where(lane == 2, ref[1], 0.0))
        for ref in (decay_own_ref, decay_other_ref)
    ]
    normed = rms_scale(seen_ref[...].astype(F32)).astype(BF16)
    weights = (
        (attend_own_ref, value_own_ref, rate_own_ref),
        (attend_other_ref, value_other_ref, rate_other_ref),
    )
    for part, (attend, value, rate) in enumerate(weights):
        proj_ref[part, :, 0:256] = dot(normed, attend[...])
        for head in range(2):
            both_parts = dot(normed, value[head])
            proj_ref[part, :, 256 + 128 * head : 384 + 128 * head] = both_parts[:, :128]
            unit = 2 * part + head
            gate_ref[:, unit * 128 : (unit + 1) * 128] = both_parts[:, 128:]
        padded = jnp.concatenate([rate[...], jnp.zeros((120, rate.shape[1]), BF16)], axis=0)
        rate_ref[part] = dot(normed, padded, ((1,), (1,)))
    for pair in range(2):
        units = []
        for traj in (2 * pair, 2 * pair + 1):
            span = slice(width * traj, width * (traj + 1))
            for part in range(2):
                query = proj_ref[part, span, 0:128]
                query = query * lax.rsqrt(jnp.sum(query * query, axis=-1, keepdims=True) + EPSILON)
                query = query * (128 ** (-0.5))
                key = proj_ref[part, span, 128:256]
                key = key * lax.rsqrt(jnp.sum(key * key, axis=-1, keepdims=True) + EPSILON)
                rates = rate_ref[part, span, :]
                plus = jnp.maximum(rates, 0.0) + jnp.log1p(jnp.exp(-jnp.abs(rates)))
                log_decay = -decays[part] * plus
                strength = jax.nn.sigmoid(rates)
                high, rest = halves(log_decay)
                low = (log_decay - high.astype(F32) - rest.astype(F32)).astype(BF16)
                summed = dot(lower3, jnp.concatenate([high, rest, low], axis=0))
                summed_rows = jnp.transpose(summed)
                products = dot(
                    left(jnp.concatenate([key, query], axis=0)), right(key, axis=1), ((1,), (1,))
                )
                for head in range(2):
                    values = proj_ref[part, span, 256 + 128 * head : 384 + 128 * head]
                    s_col = summed[:, 2 * head : 2 * head + 1]
                    s_row = summed_rows[2 * head : 2 * head + 1, :]
                    beta = strength[:, 2 * head + 1 : 2 * head + 2]
                    ratio = jnp.where(col <= row, jnp.exp(jnp.minimum(s_col - s_row, 0.0)), 0.0)
                    below = jnp.where(col < row, beta * ratio * products[:width], 0.0)
                    grown = jnp.exp(s_col)
                    units.append(
                        dict(
                            at=(traj, 2 * part + head),
                            key=key,
                            query=query,
                            s=s_col,
                            grown=grown,
                            weights=ratio * products[width:],
                            below=below,
                            below3=left(below),
                            side=jnp.concatenate([beta * values, (beta * grown) * key], axis=1),
                        )
                    )
        size = 1
        while size < width:
            corner = ((row // size) % 2 == 1) & (row // size == col // size + 1)
            corner3 = ((row3 // size) % 2 == 1) & (row3 // size == col3 // size + 1)
            if size == 1:
                for unit in units:
                    unit["inverse"] = eye - jnp.where(corner, unit["below"], 0.0)
            else:
                for unit in units:
                    step = jnp.where(corner3, unit["below3"], jnp.zeros_like(unit["below3"]))
                    unit["middle"] = dot(step, right(unit["inverse"]))
                for unit in units:
                    unit["inverse"] = unit["inverse"] - dot(
                        left(unit["inverse"]), right(unit["middle"])
                    )
            size *= 2
        for unit in units:
            unit["update"] = dot(left(unit["inverse"]), right(unit["side"]))
        for unit in units:
            traj, number = unit["at"]
            update, key, grown, s_col = unit["update"], unit["key"], unit["grown"], unit["s"]
            seen = dot(left(unit["weights"]), right(update))
            mix_ref[traj, number, 0:width, :] = update[:, 128:]
            mix_ref[traj, number, width:, :] = grown * unit["query"] - seen[:, 128:]
            base_ref[traj, number, 0:width, :] = update[:, :128]
            base_ref[traj, number, width:, :] = seen[:, :128]
            closing = s_col[width - 1 : width, :]
            key_ref[traj, number] = jnp.exp(closing - s_col) * key
            close_ref[traj, number] = jnp.broadcast_to(jnp.exp(closing), (1, 128))


def state_kernel(
    resume_ref, spot_ref, gate_ref, mix_ref, base_ref, key_ref, close_ref, held_ref, sent_ref, out_own_ref,
    out_other_ref, partial_ref, keep_ref, give_ref, gated_ref,
):
    width = 64
    for traj in range(4):
        span = slice(width * traj, width * (traj + 1))
        to_place = (spot_ref[2] + 4 - traj) % 4
        from_slot = resume_ref[spot_ref[0] * 8 + spot_ref[1] * 4 + to_place] // 8
        for part in range(2):
            for head in range(2):
                unit = part * 2 + head
                state = held_ref[from_slot, head] if part == 0 else sent_ref[from_slot, head]
                high, low = halves(mix_ref[traj, unit])
                mixed = dot(
                    jnp.concatenate([high, low], axis=1),
                    jnp.concatenate([state, state], axis=1),
                    ((1,), (1,)),
                )
                update = base_ref[traj, unit, 0:width, :] - mixed[:width]
                read = base_ref[traj, unit, width:, :] + mixed[width:]
                high, low = halves(update)
                final = close_ref[traj, unit] * state.astype(F32) + dot(
                    jnp.concatenate([high, low, high], axis=0), right(key_ref[traj, unit]), ((0,), (0,))
                )
                (keep_ref if part == 0 else give_ref)[to_place, head] = final
                gate = gate_ref[span, 128 * unit : 128 * (unit + 1)]
                gated_ref[span, 128 * unit : 128 * (unit + 1)] = (
                    rms_scale(read) * (gate * jax.nn.sigmoid(gate))
                ).astype(BF16)
    partial_ref[...] = (
        dot(gated_ref[:, 0:256], out_own_ref[...]) + dot(gated_ref[:, 256:512], out_other_ref[...])
    ).astype(BF16)


def expert_kernel(
    mine_ref, first_ref, second_ref, third_ref, fourth_ref, share_ref, inner_own_ref, outer_own_ref,
    inner_other_ref, outer_other_ref, out_ref,
):
    rows = jnp.concatenate(
        [first_ref[...], second_ref[...], third_ref[...], fourth_ref[...]], axis=0
    )
    column = lax.broadcasted_iota(jnp.int32, share_ref.shape, 1)
    total = None
    for number, inner, outer in (
        (mine_ref[0], inner_own_ref, outer_own_ref),
        (mine_ref[0] ^ 1, inner_other_ref, outer_other_ref),
    ):
        half = outer.shape[0]
        gate = dot(rows, inner[:, :half])
        up = dot(rows, inner[:, half:])
        activated = (gate * jax.nn.sigmoid(gate) * up).astype(BF16)
        produced = dot(activated, outer[...]).astype(BF16).astype(F32)
        weight = jnp.sum(jnp.where(column == number, share_ref[...], 0.0), axis=1, keepdims=True)
        total = weight * produced if total is None else total + weight * produced
    out_ref[...] = total.astype(BF16)


def local(
    tokens,
    attend_weight,
    value_weight,
    rate_weight,
    decay_rate,
    output_weight,
    state_cache,
    resume_from,
    expert_index,
    route_weight,
    expert_inner,
    expert_outer,
):
    rows, model = tokens.shape
    both = 2 * rows
    trajs = state_cache.shape[0]
    groups = lax.axis_size("rep")
    me = lax.axis_index("rep")
    mine = lax.axis_index("exp")
    my_core = mine % NC
    my_x = (mine // NC) % NX
    first = my_core == 0

    def swap(values):
        return lax.ppermute(values, "exp", SWAP)

    def in_order(own, other):
        return jnp.where(
            first, jnp.concatenate([own, other], axis=0), jnp.concatenate([other, own], axis=0)
        )

    def spread_all(values):
        return [lax.ppermute(values, "exp", spread(dx)) for dx in range(NX)]

    spot = jnp.stack([me, my_core, my_x]).astype(jnp.int32)

    token_rows = in_order(tokens, swap(tokens))
    pieces = spread_all(token_rows)

    heads, dv, dk = state_cache.shape[1:]
    slots = pl.pallas_call(
        send_kernel,
        grid_spec=pltpu.PrefetchScalarGridSpec(
            num_scalar_prefetch=2,
            grid=(1,),
            in_specs=[pl.BlockSpec((trajs, heads, dv, dk), lambda i, r, m: (0, 0, 0, 0))],
            out_specs=pl.BlockSpec((groups, heads, dv, dk), lambda i, r, m: (0, 0, 0, 0)),
        ),
        out_shape=jax.ShapeDtypeStruct((groups, heads, dv, dk), BF16),
    )(resume_from, spot, state_cache)
    arrived = lax.all_to_all(slots, "rep", split_axis=0, concat_axis=0, tiled=True)

    attend_own = attend_weight.reshape(model, -1)
    attend_other = swap(attend_own)
    token_rows, value_weight, rate_weight = lax.optimization_barrier(
        (token_rows, value_weight, rate_weight)
    )
    value_own = jnp.transpose(value_weight, (1, 0, 2))
    rate_own = jnp.pad(jnp.transpose(rate_weight, (1, 2, 0)).reshape(2 * heads, model), ((0, 4), (0, 0)))
    value_other, rate_other = swap(value_own), swap(rate_own)
    decay_other = swap(decay_rate)
    out_own = output_weight.reshape(-1, model)
    out_other = swap(out_own)
    inner_own, outer_own = expert_inner[0], expert_outer[0]
    inner_other, outer_other = swap(inner_own), swap(outer_own)

    experts = lax.axis_size("exp")
    share = jnp.sum(
        jnp.where(
            expert_index[:, :, None] == jnp.arange(experts, dtype=jnp.int32), route_weight[:, :, None], 0.0
        ),
        axis=1,
    )
    share = jnp.pad(share, ((0, 0), (0, 128 - experts)))
    shares = jnp.concatenate(spread_all(in_order(share, swap(share))), axis=0)

    gathered = jnp.concatenate(pieces, axis=0)
    vmem = pl.BlockSpec(memory_space=pltpu.VMEM)
    smem = pl.BlockSpec(memory_space=pltpu.SMEM)
    mix, base, keys, close, gates = pl.pallas_call(
        chunk_kernel,
        in_specs=[smem] * 2 + [vmem] * 7,
        out_specs=[vmem] * 5,
        out_shape=[
            jax.ShapeDtypeStruct((NX, 4, 128, 128), F32),
            jax.ShapeDtypeStruct((NX, 4, 128, 128), F32),
            jax.ShapeDtypeStruct((NX, 4, 64, 128), F32),
            jax.ShapeDtypeStruct((NX, 4, 1, 128), F32),
            jax.ShapeDtypeStruct((NX * both, 512), F32),
        ],
        scratch_shapes=[
            pltpu.VMEM((2, NX * both, 512), F32),
            pltpu.VMEM((2, NX * both, 128), F32),
        ],
    )(
        decay_rate, decay_other, gathered, attend_own, value_own, rate_own, attend_other,
        value_other, rate_other,
    )

    mix, arrived, shares = lax.optimization_barrier((mix, arrived, shares))
    from_other = swap(arrived)
    partial, keep, give = pl.pallas_call(
        state_kernel,
        in_specs=[smem] * 2 + [vmem] * 9,
        out_specs=[vmem] * 3,
        out_shape=[
            jax.ShapeDtypeStruct((NX * both, model), BF16),
            jax.ShapeDtypeStruct((NX, 2, 128, 128), F32),
            jax.ShapeDtypeStruct((NX, 2, 128, 128), F32),
        ],
        scratch_shapes=[pltpu.VMEM((NX * both, 512), BF16)],
    )(resume_from, spot, gates, mix, base, keys, close, arrived, from_other, out_own, out_other)
    final_state = in_order(keep, swap(give))

    def gather_sum(values):
        parts = [
            lax.ppermute(values[dx * both : (dx + 1) * both], "exp", collect(dx)) for dx in range(NX)
        ]
        total = parts[0].astype(F32)
        for part in parts[1:]:
            total = total + part.astype(F32)
        return total

    attended = gather_sum(partial)
    attended = attended + swap(attended.astype(BF16)).astype(F32)
    hidden = token_rows.astype(F32) + attended
    hidden_normed = rms_scale(hidden).astype(BF16)

    seen = spread_all(hidden_normed)
    mixture = pl.pallas_call(
        expert_kernel,
        in_specs=[smem] + [vmem] * 9,
        out_specs=vmem,
        out_shape=jax.ShapeDtypeStruct((NX * both, model), BF16),
    )(mine.astype(jnp.int32).reshape(1), *seen, shares, inner_own, outer_own, inner_other, outer_other)
    summed = gather_sum(mixture)
    mine_rows = jnp.where(first, summed[:rows], summed[rows:])
    others_rows = jnp.where(first, summed[rows:], summed[:rows])
    hidden_rows = jnp.where(first, hidden[:rows], hidden[rows:])
    layer_output = hidden_rows + (mine_rows + swap(others_rows.astype(BF16)).astype(F32))
    return (layer_output.astype(BF16), final_state)


def solution(mesh):
    in_specs = (
        P(("rep", "exp"), None),
        P(None, "exp", None),
        P(None, "exp", None),
        P(None, "exp", None),
        P("exp"),
        P("exp", None, None),
        P("rep", "exp", None, None),
        P(),
        P(("rep", "exp"), None),
        P(("rep", "exp"), None),
        P("exp", None, None),
        P("exp", None, None),
    )
    out_specs = (P(("rep", "exp"), None), P("rep", "exp", None, None))
    return jax.shard_map(local, mesh=mesh, in_specs=in_specs, out_specs=out_specs, check_vma=False)
```

```python
import jax
import jax.numpy as jnp
from jax import lax
from jax.experimental import pallas as pl
from jax.experimental.pallas import tpu as pltpu
from jax.sharding import PartitionSpec as P


EPSILON = 1e-06
F32 = jnp.float32
BF16 = jnp.bfloat16

NY, NX, NC = 2, 4, 2


def place(y, x, c):
    return (y * NX + x) * NC + c


SWAP = [(i, i ^ 1) for i in range(NY * NX * NC)]


def spread(dx):
    return [
        (place(y, x, c), place(y ^ c, (x + dx) % NX, y))
        for y in range(NY)
        for x in range(NX)
        for c in range(NC)
    ]


def collect(dx):
    return [(b, a) for a, b in spread(dx)]


def on_chip(values):
    return pltpu.with_memory_space_constraint(values, pltpu.VMEM)


def rms_scale(values):
    return values * lax.rsqrt(jnp.mean(values * values, axis=-1, keepdims=True) + EPSILON)


def halves(values):
    high = values.astype(BF16)
    return high, (values - high.astype(F32)).astype(BF16)


def left(values):
    high, low = halves(values)
    return jnp.concatenate([high, low, high], axis=1)


def right(values, axis=0):
    high, low = halves(values)
    return jnp.concatenate([high, high, low], axis=axis)


def dot(a, b, dims=((1,), (0,))):
    return lax.dot_general(a, b, (dims, ((), ())), preferred_element_type=F32)


def send_kernel(resume_ref, cache_ref, out_ref, short_ref, sems):
    trajs, slots = cache_ref.shape[0], out_ref.shape[0]
    me = lax.axis_index("rep")
    for row in range(trajs):
        short_ref[row] = cache_ref[row].astype(BF16)
    copies = []
    for slot in range(slots):
        row = jnp.int32(0)
        for place_of in range(trajs):
            value = resume_ref[slot * trajs + place_of]
            row = jnp.where(value // trajs == me, value % trajs, row)
        copies.append(pltpu.make_async_copy(short_ref.at[row], out_ref.at[slot], sems.at[slot]))
        copies[-1].start()
    for copy in copies:
        copy.wait()


def chunk_kernel(
    decay_own_ref, decay_other_ref, first_ref, second_ref, third_ref, fourth_ref, attend_own_ref, value_own_ref, rate_own_ref,
    attend_other_ref, value_other_ref, rate_other_ref,
    mix_ref, base_ref, key_ref, close_ref, gate_ref, proj_ref, rate_ref,
):
    width = 64
    row = lax.broadcasted_iota(jnp.int32, (width, width), 0)
    col = lax.broadcasted_iota(jnp.int32, (width, width), 1)
    row3 = lax.broadcasted_iota(jnp.int32, (width, 3 * width), 0)
    col3 = lax.broadcasted_iota(jnp.int32, (width, 3 * width), 1) % width
    lower3 = (col3 <= row3).astype(F32).astype(BF16)
    eye = (col == row).astype(F32)
    lane = lax.broadcasted_iota(jnp.int32, (1, 128), 1)
    decays = [
        jnp.where(lane == 0, ref[0], jnp.where(lane == 2, ref[1], 0.0))
        for ref in (decay_own_ref, decay_other_ref)
    ]
    normed = jnp.concatenate(
        [
            rms_scale(ref[...].astype(F32)).astype(BF16)
            for ref in (first_ref, second_ref, third_ref, fourth_ref)
        ],
        axis=0,
    )
    weights = (
        (attend_own_ref, value_own_ref, rate_own_ref),
        (attend_other_ref, value_other_ref, rate_other_ref),
    )
    for part, (attend, value, rate) in enumerate(weights):
        proj_ref[part, :, 0:256] = dot(normed, attend[...])
        for head in range(2):
            both_parts = dot(normed, value[head])
            proj_ref[part, :, 256 + 128 * head : 384 + 128 * head] = both_parts[:, :128]
            unit = 2 * part + head
            gate_ref[:, unit * 128 : (unit + 1) * 128] = both_parts[:, 128:]
        padded = jnp.concatenate([rate[...], jnp.zeros((120, rate.shape[1]), BF16)], axis=0)
        rate_ref[part] = dot(normed, padded, ((1,), (1,)))
    for pair in range(2):
        units = []
        for traj in (2 * pair, 2 * pair + 1):
            span = slice(width * traj, width * (traj + 1))
            for part in range(2):
                query = proj_ref[part, span, 0:128]
                query = query * lax.rsqrt(jnp.sum(query * query, axis=-1, keepdims=True) + EPSILON)
                query = query * (128 ** (-0.5))
                key = proj_ref[part, span, 128:256]
                key = key * lax.rsqrt(jnp.sum(key * key, axis=-1, keepdims=True) + EPSILON)
                rates = rate_ref[part, span, :]
                plus = jnp.maximum(rates, 0.0) + jnp.log1p(jnp.exp(-jnp.abs(rates)))
                log_decay = -decays[part] * plus
                strength = jax.nn.sigmoid(rates)
                high, rest = halves(log_decay)
                low = (log_decay - high.astype(F32) - rest.astype(F32)).astype(BF16)
                summed = dot(lower3, jnp.concatenate([high, rest, low], axis=0))
                summed_rows = jnp.transpose(summed)
                products = dot(
                    left(jnp.concatenate([key, query], axis=0)), right(key, axis=1), ((1,), (1,))
                )
                for head in range(2):
                    values = proj_ref[part, span, 256 + 128 * head : 384 + 128 * head]
                    s_col = summed[:, 2 * head : 2 * head + 1]
                    s_row = summed_rows[2 * head : 2 * head + 1, :]
                    beta = strength[:, 2 * head + 1 : 2 * head + 2]
                    ratio = jnp.where(col <= row, jnp.exp(jnp.minimum(s_col - s_row, 0.0)), 0.0)
                    below = jnp.where(col < row, beta * ratio * products[:width], 0.0)
                    grown = jnp.exp(s_col)
                    units.append(
                        dict(
                            at=(traj, 2 * part + head),
                            key=key,
                            query=query,
                            s=s_col,
                            grown=grown,
                            weights=ratio * products[width:],
                            below=below,
                            below3=left(below),
                            side=jnp.concatenate([beta * values, (beta * grown) * key], axis=1),
                        )
                    )
        size = 1
        while size < width:
            corner = ((row // size) % 2 == 1) & (row // size == col // size + 1)
            corner3 = ((row3 // size) % 2 == 1) & (row3 // size == col3 // size + 1)
            if size == 1:
                for unit in units:
                    unit["inverse"] = eye - jnp.where(corner, unit["below"], 0.0)
            else:
                for unit in units:
                    step = jnp.where(corner3, unit["below3"], jnp.zeros_like(unit["below3"]))
                    unit["middle"] = dot(step, right(unit["inverse"]))
                for unit in units:
                    unit["inverse"] = unit["inverse"] - dot(
                        left(unit["inverse"]), right(unit["middle"])
                    )
            size *= 2
        for unit in units:
            unit["update"] = dot(left(unit["inverse"]), right(unit["side"]))
        for unit in units:
            traj, number = unit["at"]
            update, key, grown, s_col = unit["update"], unit["key"], unit["grown"], unit["s"]
            seen = dot(left(unit["weights"]), right(update))
            mix_ref[traj, number, 0:width, :] = update[:, 128:]
            mix_ref[traj, number, width:, :] = grown * unit["query"] - seen[:, 128:]
            base_ref[traj, number, 0:width, :] = update[:, :128]
            base_ref[traj, number, width:, :] = seen[:, :128]
            closing = s_col[width - 1 : width, :]
            key_ref[traj, number] = jnp.exp(closing - s_col) * key
            close_ref[traj, number] = jnp.broadcast_to(jnp.exp(closing), (1, 128))


def state_kernel(
    resume_ref, spot_ref, gate_ref, mix_ref, base_ref, key_ref, close_ref, held_ref, sent_ref, out_own_ref,
    out_other_ref, first_ref, second_ref, third_ref, fourth_ref, keep_ref, give_ref, gated_ref,
):
    width = 64
    for traj in range(4):
        span = slice(width * traj, width * (traj + 1))
        to_place = (spot_ref[2] + 4 - traj) % 4
        from_slot = resume_ref[spot_ref[0] * 8 + spot_ref[1] * 4 + to_place] // 8
        for part in range(2):
            for head in range(2):
                unit = part * 2 + head
                state = held_ref[from_slot, head] if part == 0 else sent_ref[from_slot, head]
                high, low = halves(mix_ref[traj, unit])
                mixed = dot(
                    jnp.concatenate([high, low], axis=1),
                    jnp.concatenate([state, state], axis=1),
                    ((1,), (1,)),
                )
                update = base_ref[traj, unit, 0:width, :] - mixed[:width]
                read = base_ref[traj, unit, width:, :] + mixed[width:]
                high, low = halves(update)
                final = close_ref[traj, unit] * state.astype(F32) + dot(
                    jnp.concatenate([high, low, high], axis=0), right(key_ref[traj, unit]), ((0,), (0,))
                )
                (keep_ref if part == 0 else give_ref)[to_place, head] = final
                gate = gate_ref[span, 128 * unit : 128 * (unit + 1)]
                gated_ref[span, 128 * unit : 128 * (unit + 1)] = (
                    rms_scale(read) * (gate * jax.nn.sigmoid(gate))
                ).astype(BF16)
    partial = (
        dot(gated_ref[:, 0:256], out_own_ref[...]) + dot(gated_ref[:, 256:512], out_other_ref[...])
    ).astype(BF16)
    for traj, ref in enumerate((first_ref, second_ref, third_ref, fourth_ref)):
        ref[...] = partial[width * traj : width * (traj + 1)]


def expert_kernel(
    mine_ref, first_ref, second_ref, third_ref, fourth_ref, share_ref, inner_own_ref, outer_own_ref,
    inner_other_ref, outer_other_ref, *rest,
):
    *out_refs, inner_ref, outer_ref, sems = rest
    fetches = [
        pltpu.make_async_copy(inner_own_ref, inner_ref, sems.at[0]),
        pltpu.make_async_copy(outer_own_ref, outer_ref, sems.at[1]),
    ]
    for fetch in fetches:
        fetch.start()
    rows = jnp.concatenate(
        [first_ref[...], second_ref[...], third_ref[...], fourth_ref[...]], axis=0
    )
    column = lax.broadcasted_iota(jnp.int32, share_ref.shape, 1)
    total = None
    for number, inner, outer in (
        (mine_ref[0] ^ 1, inner_other_ref, outer_other_ref),
        (mine_ref[0], inner_ref, outer_ref),
    ):
        if total is not None:
            fetches[0].wait()
        half = outer.shape[0]
        gate = dot(rows, inner[:, :half])
        up = dot(rows, inner[:, half:])
        activated = (gate * jax.nn.sigmoid(gate) * up).astype(BF16)
        if total is not None:
            fetches[1].wait()
        produced = dot(activated, outer[...]).astype(BF16).astype(F32)
        weight = jnp.sum(jnp.where(column == number, share_ref[...], 0.0), axis=1, keepdims=True)
        total = weight * produced if total is None else total + weight * produced
    for number, ref in enumerate(out_refs):
        ref[...] = total[64 * number : 64 * (number + 1)].astype(BF16)


def local(
    tokens,
    attend_weight,
    value_weight,
    rate_weight,
    decay_rate,
    output_weight,
    state_cache,
    resume_from,
    expert_index,
    route_weight,
    expert_inner,
    expert_outer,
):
    rows, model = tokens.shape
    both = 2 * rows
    trajs = state_cache.shape[0]
    groups = lax.axis_size("rep")
    me = lax.axis_index("rep")
    mine = lax.axis_index("exp")
    my_core = mine % NC
    my_x = (mine // NC) % NX
    first = my_core == 0

    def swap(values):
        return lax.ppermute(values, "exp", SWAP)

    def in_order(own, other):
        return jnp.where(
            first, jnp.concatenate([own, other], axis=0), jnp.concatenate([other, own], axis=0)
        )

    def spread_all(values):
        return [lax.ppermute(values, "exp", spread(dx)) for dx in range(NX)]

    spot = jnp.stack([me, my_core, my_x]).astype(jnp.int32)

    heads, dv, dk = state_cache.shape[1:]
    slots = pl.pallas_call(
        send_kernel,
        in_specs=[pl.BlockSpec(memory_space=pltpu.SMEM), pl.BlockSpec(memory_space=pltpu.VMEM)],
        out_specs=pl.BlockSpec(memory_space=pl.ANY),
        out_shape=jax.ShapeDtypeStruct((groups, heads, dv, dk), BF16),
        scratch_shapes=[
            pltpu.VMEM((trajs, heads, dv, dk), BF16),
            pltpu.SemaphoreType.DMA((groups,)),
        ],
    )(resume_from, state_cache)

    tokens_other, slots = lax.optimization_barrier((swap(tokens), slots))
    arrived = lax.all_to_all(slots, "rep", split_axis=0, concat_axis=0, tiled=True)
    token_rows = in_order(tokens, tokens_other)
    pieces = []
    for dx in range(NX):
        pieces.append(lax.ppermute(token_rows, "exp", spread(dx)))

    attend_own = attend_weight.reshape(model, -1)
    rate_own = jnp.pad(jnp.transpose(rate_weight, (1, 2, 0)).reshape(2 * heads, model), ((0, 4), (0, 0)))
    rate_other = swap(rate_own)
    decay_other = swap(decay_rate)
    attend_other = swap(attend_own)
    token_rows, value_weight = lax.optimization_barrier((token_rows, value_weight))
    value_own = jnp.transpose(value_weight, (1, 0, 2))
    value_other = swap(value_own)
    out_own = output_weight.reshape(-1, model)
    inner_own, outer_own = expert_inner[0], expert_outer[0]
    experts = lax.axis_size("exp")
    share = jnp.sum(
        jnp.where(
            expert_index[:, :, None] == jnp.arange(experts, dtype=jnp.int32), route_weight[:, :, None], 0.0
        ),
        axis=1,
    )
    share = jnp.pad(share, ((0, 0), (0, 128 - experts)))
    share_other = swap(share)
    shares = jnp.concatenate(spread_all(in_order(share, share_other)), axis=0)

    *pieces, shares, rate_other, decay_other, out_sent, inner_sent, outer_sent = (
        lax.optimization_barrier(
            (*pieces, shares, rate_other, decay_other, out_own, inner_own, outer_own)
        )
    )
    out_other, inner_other, outer_other = swap(out_sent), swap(inner_sent), swap(outer_sent)

    vmem = pl.BlockSpec(memory_space=pltpu.VMEM)
    smem = pl.BlockSpec(memory_space=pltpu.SMEM)
    mix, base, keys, close, gates = pl.pallas_call(
        chunk_kernel,
        in_specs=[smem] * 2 + [vmem] * 10,
        out_specs=[vmem] * 5,
        out_shape=[
            jax.ShapeDtypeStruct((NX, 4, 128, 128), F32),
            jax.ShapeDtypeStruct((NX, 4, 128, 128), F32),
            jax.ShapeDtypeStruct((NX, 4, 64, 128), F32),
            jax.ShapeDtypeStruct((NX, 4, 1, 128), F32),
            jax.ShapeDtypeStruct((NX * both, 512), F32),
        ],
        scratch_shapes=[
            pltpu.VMEM((2, NX * both, 512), F32),
            pltpu.VMEM((2, NX * both, 128), F32),
        ],
    )(
        decay_rate, decay_other, *pieces, attend_own, value_own, rate_own, attend_other,
        value_other, rate_other,
    )

    mix, arrived, shares = lax.optimization_barrier((mix, arrived, shares))
    from_other = swap(arrived)
    *partial, keep, give = pl.pallas_call(
        state_kernel,
        in_specs=[smem] * 2 + [vmem] * 9,
        out_specs=[vmem] * (NX + 2),
        out_shape=[jax.ShapeDtypeStruct((both, model), BF16)] * NX
        + [
            jax.ShapeDtypeStruct((NX, 2, 128, 128), F32),
            jax.ShapeDtypeStruct((NX, 2, 128, 128), F32),
        ],
        scratch_shapes=[pltpu.VMEM((NX * both, 512), BF16)],
    )(resume_from, spot, gates, mix, base, keys, close, arrived, from_other, out_own, out_other)
    final_state = in_order(keep, swap(give))

    def gather_sum(values):
        parts = [lax.ppermute(values[dx], "exp", collect(dx)) for dx in range(NX)]
        total = parts[0].astype(F32)
        for part in parts[1:]:
            total = total + part.astype(F32)
        return total

    attended = gather_sum(partial)
    attended = attended + swap(attended.astype(BF16)).astype(F32)
    hidden = token_rows.astype(F32) + attended
    hidden_normed = rms_scale(hidden).astype(BF16)

    seen = spread_all(hidden_normed)
    seen[0], final_state = lax.optimization_barrier((seen[0], final_state))
    hbm = pl.BlockSpec(memory_space=pl.ANY)
    mixture = pl.pallas_call(
        expert_kernel,
        in_specs=[smem] + [vmem] * 5 + [hbm] * 2 + [vmem] * 2,
        out_specs=[vmem] * NX,
        out_shape=[jax.ShapeDtypeStruct((both, model), BF16)] * NX,
        scratch_shapes=[
            pltpu.VMEM(inner_own.shape, BF16),
            pltpu.VMEM(outer_own.shape, BF16),
            pltpu.SemaphoreType.DMA((2,)),
        ],
        compiler_params=pltpu.CompilerParams(vmem_limit_bytes=28 << 20),
    )(
        mine.astype(jnp.int32).reshape(1), *map(on_chip, seen), on_chip(shares), inner_own, outer_own,
        on_chip(inner_other), on_chip(outer_other),
    )
    summed = gather_sum(mixture)
    mine_rows = jnp.where(first, summed[:rows], summed[rows:])
    others_rows = jnp.where(first, summed[rows:], summed[:rows])
    hidden_rows = jnp.where(first, hidden[:rows], hidden[rows:])
    layer_output = hidden_rows + (mine_rows + swap(others_rows.astype(BF16)).astype(F32))
    return (layer_output.astype(BF16), final_state)


def solution(mesh):
    in_specs = (
        P(("rep", "exp"), None),
        P(None, "exp", None),
        P(None, "exp", None),
        P(None, "exp", None),
        P("exp"),
        P("exp", None, None),
        P("rep", "exp", None, None),
        P(),
        P(("rep", "exp"), None),
        P(("rep", "exp"), None),
        P("exp", None, None),
        P("exp", None, None),
    )
    out_specs = (P(("rep", "exp"), None), P("rep", "exp", None, None))

    return jax.shard_map(local, mesh=mesh, in_specs=in_specs, out_specs=out_specs, check_vma=False)
```

```python
import jax
import jax.numpy as jnp
from jax import lax
from jax.experimental import pallas as pl
from jax.experimental.pallas import tpu as pltpu
from jax.sharding import PartitionSpec as P


EPSILON = 1e-06
EXPERTS = 16
F32 = jnp.float32
BF16 = jnp.bfloat16

NY, NX, NC = 2, 4, 2


def place(y, x, c):
    return (y * NX + x) * NC + c


SWAP = [(i, i ^ 1) for i in range(NY * NX * NC)]


def spread(dx):
    return [
        (place(y, x, c), place(y ^ c, (x + dx) % NX, y))
        for y in range(NY)
        for x in range(NX)
        for c in range(NC)
    ]


def collect(dx):
    return [(b, a) for a, b in spread(dx)]


def on_chip(values):
    return pltpu.with_memory_space_constraint(values, pltpu.VMEM)


def off_chip(values):
    return pltpu.with_memory_space_constraint(values, pltpu.HBM)


def rms_scale(values):
    return values * lax.rsqrt(jnp.mean(values * values, axis=-1, keepdims=True) + EPSILON)


def halves(values):
    high = values.astype(BF16)
    return high, (values - high.astype(F32)).astype(BF16)


def left(values):
    high, low = halves(values)
    return jnp.concatenate([high, low, high], axis=1)


def right(values, axis=0):
    high, low = halves(values)
    return jnp.concatenate([high, high, low], axis=axis)


def dot(a, b, dims=((1,), (0,))):
    return lax.dot_general(a, b, (dims, ((), ())), preferred_element_type=F32)


def send_kernel(resume_ref, cache_ref, out_ref, short_ref, sems):
    trajs, slots = cache_ref.shape[0], out_ref.shape[0]
    me = lax.axis_index("rep")
    for row in range(trajs):
        short_ref[row] = cache_ref[row].astype(BF16)
    copies = []
    for slot in range(slots):
        row = jnp.int32(0)
        for place_of in range(trajs):
            value = resume_ref[slot * trajs + place_of]
            row = jnp.where(value // trajs == me, value % trajs, row)
        copies.append(pltpu.make_async_copy(short_ref.at[row], out_ref.at[slot], sems.at[slot]))
        copies[-1].start()
    for copy in copies:
        copy.wait()


def chunk_kernel(
    decay_own_ref, decay_other_ref, first_ref, second_ref, third_ref, fourth_ref, attend_own_ref, value_own_ref, rate_own_ref,
    attend_other_ref, value_other_ref, rate_other_ref,
    mix_ref, base_ref, key_ref, close_ref, gate_ref, proj_ref, rate_ref,
):
    width = 64
    row = lax.broadcasted_iota(jnp.int32, (width, width), 0)
    col = lax.broadcasted_iota(jnp.int32, (width, width), 1)
    row3 = lax.broadcasted_iota(jnp.int32, (width, 3 * width), 0)
    col3 = lax.broadcasted_iota(jnp.int32, (width, 3 * width), 1) % width
    lower3 = (col3 <= row3).astype(F32).astype(BF16)
    eye = (col == row).astype(F32)
    lane = lax.broadcasted_iota(jnp.int32, (1, 128), 1)
    decays = [
        jnp.where(lane == 0, ref[0], jnp.where(lane == 2, ref[1], 0.0))
        for ref in (decay_own_ref, decay_other_ref)
    ]
    normed = jnp.concatenate(
        [
            rms_scale(ref[...].astype(F32)).astype(BF16)
            for ref in (first_ref, second_ref, third_ref, fourth_ref)
        ],
        axis=0,
    )
    weights = (
        (attend_own_ref, value_own_ref, rate_own_ref),
        (attend_other_ref, value_other_ref, rate_other_ref),
    )
    for part, (attend, value, rate) in enumerate(weights):
        proj_ref[part, :, 0:256] = dot(normed, attend[...])
        for head in range(2):
            both_parts = dot(normed, value[head])
            proj_ref[part, :, 256 + 128 * head : 384 + 128 * head] = both_parts[:, :128]
            unit = 2 * part + head
            gate_ref[:, unit * 128 : (unit + 1) * 128] = both_parts[:, 128:]
        padded = jnp.concatenate([rate[...], jnp.zeros((120, rate.shape[1]), BF16)], axis=0)
        rate_ref[part] = dot(normed, padded, ((1,), (1,)))
    for pair in range(2):
        units = []
        for traj in (2 * pair, 2 * pair + 1):
            span = slice(width * traj, width * (traj + 1))
            for part in range(2):
                query = proj_ref[part, span, 0:128]
                query = query * lax.rsqrt(jnp.sum(query * query, axis=-1, keepdims=True) + EPSILON)
                query = query * (128 ** (-0.5))
                key = proj_ref[part, span, 128:256]
                key = key * lax.rsqrt(jnp.sum(key * key, axis=-1, keepdims=True) + EPSILON)
                rates = rate_ref[part, span, :]
                plus = jnp.maximum(rates, 0.0) + jnp.log1p(jnp.exp(-jnp.abs(rates)))
                log_decay = -decays[part] * plus
                strength = jax.nn.sigmoid(rates)
                high, rest = halves(log_decay)
                low = (log_decay - high.astype(F32) - rest.astype(F32)).astype(BF16)
                summed = dot(lower3, jnp.concatenate([high, rest, low], axis=0))
                summed_rows = jnp.transpose(summed)
                products = dot(
                    left(jnp.concatenate([key, query], axis=0)), right(key, axis=1), ((1,), (1,))
                )
                for head in range(2):
                    values = proj_ref[part, span, 256 + 128 * head : 384 + 128 * head]
                    s_col = summed[:, 2 * head : 2 * head + 1]
                    s_row = summed_rows[2 * head : 2 * head + 1, :]
                    beta = strength[:, 2 * head + 1 : 2 * head + 2]
                    ratio = jnp.where(col <= row, jnp.exp(jnp.minimum(s_col - s_row, 0.0)), 0.0)
                    below = jnp.where(col < row, beta * ratio * products[:width], 0.0)
                    grown = jnp.exp(s_col)
                    units.append(
                        dict(
                            at=(traj, 2 * part + head),
                            key=key,
                            query=query,
                            s=s_col,
                            grown=grown,
                            weights=ratio * products[width:],
                            below=below,
                            below3=left(below),
                            side=jnp.concatenate([beta * values, (beta * grown) * key], axis=1),
                        )
                    )
        size = 1
        while size < width:
            corner = ((row // size) % 2 == 1) & (row // size == col // size + 1)
            corner3 = ((row3 // size) % 2 == 1) & (row3 // size == col3 // size + 1)
            if size == 1:
                for unit in units:
                    unit["inverse"] = eye - jnp.where(corner, unit["below"], 0.0)
            else:
                for unit in units:
                    step = jnp.where(corner3, unit["below3"], jnp.zeros_like(unit["below3"]))
                    unit["middle"] = dot(step, right(unit["inverse"]))
                for unit in units:
                    unit["inverse"] = unit["inverse"] - dot(
                        left(unit["inverse"]), right(unit["middle"])
                    )
            size *= 2
        for unit in units:
            unit["update"] = dot(left(unit["inverse"]), right(unit["side"]))
        for unit in units:
            traj, number = unit["at"]
            update, key, grown, s_col = unit["update"], unit["key"], unit["grown"], unit["s"]
            seen = dot(left(unit["weights"]), right(update))
            mix_ref[traj, number, 0:width, :] = update[:, 128:]
            mix_ref[traj, number, width:, :] = grown * unit["query"] - seen[:, 128:]
            base_ref[traj, number, 0:width, :] = update[:, :128]
            base_ref[traj, number, width:, :] = seen[:, :128]
            closing = s_col[width - 1 : width, :]
            key_ref[traj, number] = jnp.exp(closing - s_col) * key
            close_ref[traj, number] = jnp.broadcast_to(jnp.exp(closing), (1, 128))


def state_kernel(
    resume_ref, gate_ref, mix_ref, base_ref, key_ref, close_ref, held_ref, sent_ref, out_own_ref,
    out_other_ref, first_ref, second_ref, third_ref, fourth_ref, keep_ref, give_ref, gated_ref,
):
    width = 64
    mine = lax.axis_index("exp")
    my_core, my_x = mine % NC, (mine // NC) % NX
    for traj in range(4):
        span = slice(width * traj, width * (traj + 1))
        to_place = (my_x + 4 - traj) % 4
        from_slot = resume_ref[lax.axis_index("rep") * 8 + my_core * 4 + to_place] // 8
        for part in range(2):
            for head in range(2):
                unit = part * 2 + head
                state = held_ref[from_slot, head] if part == 0 else sent_ref[from_slot, head]
                high, low = halves(mix_ref[traj, unit])
                mixed = dot(
                    jnp.concatenate([high, low], axis=1),
                    jnp.concatenate([state, state], axis=1),
                    ((1,), (1,)),
                )
                update = base_ref[traj, unit, 0:width, :] - mixed[:width]
                read = base_ref[traj, unit, width:, :] + mixed[width:]
                high, low = halves(update)
                final = close_ref[traj, unit] * state.astype(F32) + dot(
                    jnp.concatenate([high, low, high], axis=0), right(key_ref[traj, unit]), ((0,), (0,))
                )
                (keep_ref if part == 0 else give_ref)[to_place, head] = final
                gate = gate_ref[span, 128 * unit : 128 * (unit + 1)]
                gated_ref[span, 128 * unit : 128 * (unit + 1)] = (
                    rms_scale(read) * (gate * jax.nn.sigmoid(gate))
                ).astype(BF16)
    partial = (
        dot(gated_ref[:, 0:256], out_own_ref[...]) + dot(gated_ref[:, 256:512], out_other_ref[...])
    ).astype(BF16)
    for traj, ref in enumerate((first_ref, second_ref, third_ref, fourth_ref)):
        ref[...] = partial[width * traj : width * (traj + 1)]


def expert_kernel(
    mine_ref, first_ref, second_ref, third_ref, fourth_ref, inner_own_ref, outer_own_ref,
    inner_other_ref, outer_other_ref, *rest,
):
    *out_refs, inner_ref, outer_ref, sems = rest
    fetches = [
        pltpu.make_async_copy(inner_own_ref, inner_ref, sems.at[0]),
        pltpu.make_async_copy(outer_own_ref, outer_ref, sems.at[1]),
    ]
    for fetch in fetches:
        fetch.start()
    model = inner_ref.shape[0]
    refs = (first_ref, second_ref, third_ref, fourth_ref)
    rows = jnp.concatenate([ref[:, :model] for ref in refs], axis=0)
    share = jnp.concatenate([ref[:, model:] for ref in refs], axis=0).astype(F32)
    column = lax.broadcasted_iota(jnp.int32, share.shape, 1) % EXPERTS
    total = None
    for number, inner, outer in (
        (mine_ref[0] ^ 1, inner_other_ref, outer_other_ref),
        (mine_ref[0], inner_ref, outer_ref),
    ):
        if total is not None:
            fetches[0].wait()
        half = outer.shape[0]
        gate = dot(rows, inner[:, :half])
        up = dot(rows, inner[:, half:])
        activated = (gate * jax.nn.sigmoid(gate) * up).astype(BF16)
        if total is not None:
            fetches[1].wait()
        produced = dot(activated, outer[...]).astype(BF16).astype(F32)
        weight = jnp.sum(jnp.where(column == number, share, 0.0), axis=1, keepdims=True)
        total = weight * produced if total is None else total + weight * produced
    for number, ref in enumerate(out_refs):
        ref[...] = total[64 * number : 64 * (number + 1)].astype(BF16)


def local(
    tokens,
    attend_weight,
    value_weight,
    rate_weight,
    decay_rate,
    output_weight,
    state_cache,
    resume_from,
    expert_index,
    route_weight,
    expert_inner,
    expert_outer,
):
    rows, model = tokens.shape
    both = 2 * rows
    trajs = state_cache.shape[0]
    groups = lax.axis_size("rep")
    mine = lax.axis_index("exp")
    my_core = mine % NC
    first = my_core == 0

    def swap(values):
        return lax.ppermute(values, "exp", SWAP)

    def in_order(own, other):
        return jnp.where(
            first, jnp.concatenate([own, other], axis=0), jnp.concatenate([other, own], axis=0)
        )

    def spread_all(values):
        return [lax.ppermute(values, "exp", spread(dx)) for dx in range(NX)]


    out_own = output_weight.reshape(-1, model)
    inner_own, outer_own = expert_inner[0], expert_outer[0]
    attend_own = attend_weight.reshape(model, -1)
    attend_other = swap(attend_own)
    out_other = swap(out_own)
    inner_other = swap(inner_own)
    outer_other = swap(outer_own)

    heads, dv, dk = state_cache.shape[1:]
    slots = pl.pallas_call(
        send_kernel,
        in_specs=[pl.BlockSpec(memory_space=pltpu.SMEM), pl.BlockSpec(memory_space=pltpu.VMEM)],
        out_specs=pl.BlockSpec(memory_space=pl.ANY),
        out_shape=jax.ShapeDtypeStruct((groups, heads, dv, dk), BF16),
        scratch_shapes=[
            pltpu.VMEM((trajs, heads, dv, dk), BF16),
            pltpu.SemaphoreType.DMA((groups,)),
        ],
    )(resume_from, state_cache)

    tokens_other, slots = lax.optimization_barrier((swap(tokens), slots))
    arrived = lax.all_to_all(slots, "rep", split_axis=0, concat_axis=0, tiled=True)
    token_rows = in_order(tokens, tokens_other)
    pieces = []
    for dx in range(NX):
        pieces.append(lax.ppermute(token_rows, "exp", spread(dx)))

    rate_own = jnp.transpose(rate_weight, (1, 2, 0)).reshape(2 * heads, model)
    rate_own = jnp.pad(rate_own, ((0, 8 - 2 * heads), (0, 0)))
    rate_other = swap(rate_own)
    decay_other = swap(decay_rate)
    token_rows, value_weight = lax.optimization_barrier((token_rows, value_weight))
    value_own = jnp.transpose(value_weight, (1, 0, 2))
    value_other = swap(value_own)
    share = jnp.sum(
        jnp.where(
            expert_index[:, :, None] == jnp.arange(EXPERTS, dtype=jnp.int32),
            route_weight[:, :, None],
            0.0,
        ),
        axis=1,
    )
    high, rest = halves(share)
    low = (share - high.astype(F32) - rest.astype(F32)).astype(BF16)
    share = jnp.concatenate([high, rest, low, jnp.zeros((rows, 128 - 3 * EXPERTS), BF16)], axis=1)
    share_other = swap(share)
    share_rows = in_order(share, share_other)

    vmem = pl.BlockSpec(memory_space=pltpu.VMEM)
    smem = pl.BlockSpec(memory_space=pltpu.SMEM)
    mix, base, keys, close, gates = pl.pallas_call(
        chunk_kernel,
        in_specs=[smem] * 2 + [vmem] * 10,
        out_specs=[vmem] * 5,
        out_shape=[
            pltpu.HBM((NX, 4, 128, 128), F32),
            pltpu.HBM((NX, 4, 128, 128), F32),
            pltpu.HBM((NX, 4, 64, 128), F32),
            pltpu.HBM((NX, 4, 1, 128), F32),
            pltpu.HBM((NX * both, 512), F32),
        ],
        scratch_shapes=[
            pltpu.VMEM((2, NX * both, 512), F32),
            pltpu.VMEM((2, NX * both, 128), F32),
        ],
        compiler_params=pltpu.CompilerParams(vmem_limit_bytes=24 << 20),
    )(
        decay_rate, decay_other, *pieces, attend_own, on_chip(value_own), rate_own,
        on_chip(attend_other), on_chip(value_other), rate_other,
    )

    mix, arrived, share_rows = lax.optimization_barrier((mix, arrived, share_rows))
    from_other = swap(arrived)
    *partial, keep, give = pl.pallas_call(
        state_kernel,
        in_specs=[smem] + [vmem] * 9,
        out_specs=[vmem] * (NX + 2),
        out_shape=[jax.ShapeDtypeStruct((both, model), BF16)] * NX
        + [
            jax.ShapeDtypeStruct((NX, 2, 128, 128), F32),
            jax.ShapeDtypeStruct((NX, 2, 128, 128), F32),
        ],
        scratch_shapes=[pltpu.VMEM((NX * both, 512), BF16)],
        compiler_params=pltpu.CompilerParams(vmem_limit_bytes=20 << 20),
    )(
        resume_from, *map(off_chip, (gates, mix, base, keys, close)), on_chip(arrived),
        on_chip(from_other), off_chip(out_own), off_chip(out_other),
    )
    final_state = in_order(keep, swap(give))

    def gather_sum(values):
        parts = [lax.ppermute(values[dx], "exp", collect(dx)) for dx in range(NX)]
        total = parts[0].astype(F32)
        for part in parts[1:]:
            total = total + part.astype(F32)
        return total

    attended = gather_sum(partial)
    attended = attended + swap(attended.astype(BF16)).astype(F32)
    hidden = token_rows.astype(F32) + attended
    hidden_normed = rms_scale(hidden).astype(BF16)

    hbm = pl.BlockSpec(memory_space=pl.ANY)
    seen = spread_all(jnp.concatenate([hidden_normed, share_rows], axis=1))
    seen[0], final_state = lax.optimization_barrier((seen[0], final_state))
    mixture = pl.pallas_call(
        expert_kernel,
        in_specs=[smem] + [vmem] * 4 + [hbm] * 2 + [vmem] * 2,
        out_specs=[vmem] * NX,
        out_shape=[jax.ShapeDtypeStruct((both, model), BF16)] * NX,
        scratch_shapes=[
            pltpu.VMEM(inner_own.shape, BF16),
            pltpu.VMEM(outer_own.shape, BF16),
            pltpu.SemaphoreType.DMA((2,)),
        ],
        compiler_params=pltpu.CompilerParams(vmem_limit_bytes=28 << 20),
    )(
        mine.astype(jnp.int32).reshape(1), *map(on_chip, seen), inner_own, outer_own,
        on_chip(inner_other), on_chip(outer_other),
    )
    summed = gather_sum(mixture)
    mine_rows = jnp.where(first, summed[:rows], summed[rows:])
    others_rows = jnp.where(first, summed[rows:], summed[:rows])
    hidden_rows = jnp.where(first, hidden[:rows], hidden[rows:])
    layer_output = hidden_rows + (mine_rows + swap(others_rows.astype(BF16)).astype(F32))
    return (layer_output.astype(BF16), final_state)


def solution(mesh):
    in_specs = (
        P(("rep", "exp"), None),
        P(None, "exp", None),
        P(None, "exp", None),
        P(None, "exp", None),
        P("exp"),
        P("exp", None, None),
        P("rep", "exp", None, None),
        P(),
        P(("rep", "exp"), None),
        P(("rep", "exp"), None),
        P("exp", None, None),
        P("exp", None, None),
    )
    out_specs = (P(("rep", "exp"), None), P("rep", "exp", None, None))

    return jax.shard_map(local, mesh=mesh, in_specs=in_specs, out_specs=out_specs, check_vma=False)
```
